256 devices in a mesh: orbit: 16 (over y_hi, x, core), tile: 16 (over y_lo, z).
Axes of the slice: x: 4, y: 4 (y_hi: 2, y_lo: 2; y = y_hi * 2 + y_lo), z: 8, core: 2. Of those that a mesh axis runs over, the one named last changes fastest.
Arguments:
- tokens: bfloat16 [64, 1024, 1280], P('orbit', 'tile'), may hold values from -6 to 6
- cotangent: bfloat16 [64, 1024, 1280], P('orbit', 'tile'), may hold values from -60 to 60
- w_query: bfloat16 [1280, 1280], replicated, may hold values from -0.15625 to 0.15625
- w_key: bfloat16 [1280, 1280], replicated, may hold values from -0.15625 to 0.15625
- w_value: bfloat16 [1280, 1280], replicated, may hold values from -0.15625 to 0.15625
- conv_taps: float32 [3, 1280], replicated, may hold values from 0.3 to 1
- conv_bias: float32 [1280], replicated, may hold values from -2 to 2
Outputs:
- grad_tokens: bfloat16 [64, 1024, 1280], P('orbit', 'tile')
The draws below stay inside these ranges and needn't reach their ends.
All inputs are finite; a program needn't handle non-finite values.
Results may differ from the reference program's by a relative error of at most 0.009.
The reference program's roundings to bfloat16 on the way count: a program that leaves them out, or rounds other values in their place, can miss the bound.
Values may be sent and summed in bfloat16 or wider, within the bound.
A program may use at most 64 MiB of HBM per device.

```python
import math
import jax
import jax.numpy as jnp
from jax import lax

C = 1280
HEAD_DIM = 64
TOK_DEV = 64
FRAMES = 64
SPATIAL = 1024
N_TILE = 16


def draw_tokens(key, part):
    keys_split = jax.random.split(key, 1)
    sample = jax.random.normal(keys_split[0], (FRAMES, SPATIAL, C), jnp.float32)
    return jnp.clip(sample, -6.0, 6.0).astype(jnp.bfloat16)


def draw_cotangent(key, part):
    keys_split = jax.random.split(key, 4)
    position = jnp.arange(SPATIAL, dtype=jnp.float32) / SPATIAL
    row_jitter = jax.random.uniform(keys_split[1], (SPATIAL,), jnp.float32, -0.5, 0.5)
    row_level = jnp.exp(math.log(10.0) * position + row_jitter)[None, :, None]
    column_level = 0.3 * jnp.exp(jax.random.uniform(keys_split[2], (C,), jnp.float32, 0.0, math.log(10.0)))[None, None, :]
    frame_level = jnp.exp(jax.random.uniform(keys_split[3], (FRAMES,), jnp.float32, -0.5, 0.5))[:, None, None]
    sample = jnp.clip(jax.random.normal(keys_split[0], (FRAMES, SPATIAL, C), jnp.float32), -3.0, 3.0)
    return jnp.clip(sample * row_level * column_level * frame_level, -60.0, 60.0).astype(jnp.bfloat16)


def bell_draw(stream_key, extent, width, limit, held_as=jnp.bfloat16):
    entries = jax.random.normal(stream_key, extent, jnp.float32) * width
    return jnp.minimum(jnp.maximum(entries, -limit), limit).astype(held_as)


def setup_inputs(seed: int = 0) -> dict:
    streams_of = jax.random.split(jax.random.key(seed), 8)
    return {
        "tokens": draw_tokens(jax.random.fold_in(streams_of[7], 71), 0),
        "cotangent": draw_cotangent(jax.random.fold_in(streams_of[7], 71), 0),
        "w_query": bell_draw(streams_of[2], (C, C), C ** -0.5, 0.15625),
        "w_key": bell_draw(streams_of[3], (C, C), C ** -0.5, 0.15625),
        "w_value": bell_draw(streams_of[4], (C, C), C ** -0.5, 0.15625),
        "conv_taps": jnp.clip(jnp.exp(jax.random.uniform(streams_of[5], (3, C), jnp.float32, math.log(0.3), math.log(1.0))), 0.3, 1.0),
        "conv_bias": bell_draw(streams_of[6], (C,), 0.5, 2.0, jnp.float32),
    }


def round_trip(signal):
    return lax.optimization_barrier(signal.astype(jnp.bfloat16)).astype(jnp.float32)

def temporal_mix(signal, conv_taps):
    return conv_taps[0] * jnp.roll(signal, 1, axis=0) + conv_taps[1] * signal + conv_taps[2] * jnp.roll(signal, -1, axis=0)

def temporal_unmix(signal, conv_taps):
    return signal + conv_taps[0] * jnp.roll(signal, -1, axis=0) + conv_taps[1] * signal + conv_taps[2] * jnp.roll(signal, 1, axis=0)

def attention_grads(query_rows, key_rows, value_rows, grad_rows):
    frames, tok_count, channels = query_rows.shape
    head_count = channels // HEAD_DIM
    inv_root = 1.0 / math.sqrt(HEAD_DIM)
    shape_heads = (frames, tok_count, head_count, HEAD_DIM)
    q_heads = query_rows.astype(jnp.float32).reshape(shape_heads)
    k_heads = key_rows.astype(jnp.float32).reshape(shape_heads)
    v_heads = value_rows.astype(jnp.float32).reshape(shape_heads)
    g_heads = grad_rows.astype(jnp.float32).reshape(shape_heads)
    scores = jnp.einsum('fshd,gshd->shfg', q_heads, k_heads) * inv_root
    peak = lax.optimization_barrier(jnp.max(scores, axis=-1, keepdims=True))
    expo_terms = jnp.exp(scores - peak)
    attn_prob = expo_terms / lax.optimization_barrier(jnp.sum(expo_terms, axis=-1, keepdims=True))
    prob_low = round_trip(attn_prob)
    attn_out = jnp.einsum('shfg,gshd->fshd', prob_low, v_heads)
    row_delta = lax.optimization_barrier(jnp.sum(g_heads * attn_out, axis=-1))
    grad_value = jnp.einsum('shfg,fshd->gshd', prob_low, g_heads).astype(jnp.bfloat16)
    grad_prob = jnp.einsum('fshd,gshd->shfg', g_heads, v_heads)
    d_scores = attn_prob * (grad_prob - jnp.transpose(row_delta, (1, 2, 0))[..., None])
    scores_low = round_trip(d_scores)
    grad_query = (jnp.einsum('shfg,gshd->fshd', scores_low, k_heads) * inv_root).astype(jnp.bfloat16)
    grad_key = (jnp.einsum('shfg,fshd->gshd', scores_low, q_heads) * inv_root).astype(jnp.bfloat16)
    full_shape = (frames, tok_count, channels)
    return (grad_query.reshape(full_shape), grad_key.reshape(full_shape), grad_value.reshape(full_shape))

def attend_block(block):
    return attention_grads(block[0], block[1], block[2], block[3])

def reference(tokens, cotangent, w_query, w_key, w_value, conv_taps, conv_bias):
    frames, spatial, channels = tokens.shape
    source = tokens.astype(jnp.float32)
    hidden = (source + temporal_mix(source, conv_taps) + conv_bias).astype(jnp.bfloat16)
    flat_rows = hidden.reshape(frames * spatial, channels)
    projected = tuple((jnp.dot(flat_rows, weight, preferred_element_type=jnp.float32).astype(jnp.bfloat16).reshape(frames, spatial, channels) for weight in (w_query, w_key, w_value)))
    grad_f = cotangent.astype(jnp.float32)
    energy = lax.optimization_barrier(jnp.sum(grad_f * grad_f, axis=(1, 2)))
    factor = lax.rsqrt(energy / (spatial * channels) + 1e-06)
    grad_out = (grad_f * factor[:, None, None]).astype(jnp.bfloat16)
    stacked = tuple((jnp.moveaxis(member.reshape(frames, N_TILE, TOK_DEV, channels), 1, 0) for member in (projected[0], projected[1], projected[2], grad_out)))
    results = lax.map(attend_block, stacked)
    grads = tuple((jnp.moveaxis(member, 0, 1).reshape(frames * spatial, channels) for member in results))
    grad_hidden = (jnp.dot(grads[0], w_query.T, preferred_element_type=jnp.float32) + jnp.dot(grads[1], w_key.T, preferred_element_type=jnp.float32) + jnp.dot(grads[2], w_value.T, preferred_element_type=jnp.float32)).astype(jnp.bfloat16)
    grad_field = grad_hidden.reshape(frames, spatial, channels).astype(jnp.float32)
    return temporal_unmix(grad_field, conv_taps).astype(jnp.bfloat16)
```

```python
import functools

import jax
import jax.numpy as jnp
from jax import lax
from jax.experimental import pallas as pl
from jax.experimental.pallas import tpu as pltpu
from jax.sharding import PartitionSpec as P

MESH = pl.DeviceIdType.MESH
HEAD_DIM = 64
PAIR = 2 * HEAD_DIM
SCALE = HEAD_DIM**-0.5
GROUP = 16
HALVES = 2
CHUNK = 8
ROWS = GROUP * CHUNK
BF16 = jnp.bfloat16
F32 = jnp.float32


def partner_of(me, k):
    core, x, y = me % 2, (me // 2) % 4, me // 8
    return ((y + k // 8) % 2) * 8 + ((x + (k // 2) % 4) % 4) * 2 + (core + k % 2) % 2


def source_of(me, k):
    core, x, y = me % 2, (me // 2) % 4, me // 8
    return ((y + k // 8) % 2) * 8 + ((x + 4 - (k // 2) % 4) % 4) * 2 + (core + k % 2) % 2


def one_hot(source):
    columns = lax.broadcasted_iota(jnp.int32, (ROWS, ROWS), 1)
    return jnp.where(columns == source, 1.0, 0.0).astype(BF16)


def row_index():
    return lax.broadcasted_iota(jnp.int32, (ROWS, ROWS), 0)


def dot(a, b, dims=((1,), (0,))):
    return lax.dot_general(a, b, (dims, ((), ())), preferred_element_type=F32)


def stacked(block):
    lanes = lax.broadcasted_iota(jnp.int32, block.shape, 1)
    zero = jnp.zeros_like(block)
    return jnp.concatenate(
        [jnp.where(lanes < HEAD_DIM, block, zero), jnp.where(lanes < HEAD_DIM, zero, block)], axis=0
    )


def kernel(
    comm,
    tokens_hbm,
    cot_hbm,
    wq_hbm,
    wk_hbm,
    wv_hbm,
    taps_ref,
    bias_ref,
    out_ref,
    tok_in,
    cot_in,
    w,
    tsend,
    trecv,
    csend,
    crecv,
    gsend,
    grecv,
    esend,
    erecv,
    fsend,
    frecv,
    hid,
    qkv,
    qs_all,
    probs,
    grads,
    ghid,
    load_sem,
    send_sem,
    recv_sem,
):
    me = lax.axis_index("orbit")
    tile = lax.axis_index("tile")
    channels = tok_in.shape[-1]
    barrier = pltpu.get_barrier_semaphore()
    if comm:
        for k in range(1, GROUP):
            pl.semaphore_signal(barrier, inc=1, device_id=((me + k) % GROUP, tile), device_id_type=MESH)
            pl.semaphore_signal(barrier, inc=1, device_id=(me, (tile + k) % GROUP), device_id_type=MESH)
    loads = [
        pltpu.make_async_copy(tokens_hbm, tok_in, load_sem.at[0]),
        pltpu.make_async_copy(cot_hbm, cot_in, load_sem.at[1]),
        pltpu.make_async_copy(wq_hbm, w.at[0], load_sem.at[2]),
        pltpu.make_async_copy(wk_hbm, w.at[1], load_sem.at[3]),
        pltpu.make_async_copy(wv_hbm, w.at[2], load_sem.at[4]),
    ]
    for load in loads:
        load.start()

    rows = row_index()
    half_tokens = tok_in.shape[1] // HALVES
    to_chunks = one_hot((rows & 3) * half_tokens + (rows >> 3) * 2 + ((rows >> 2) & 1))
    from_chunks = one_hot(((rows % half_tokens) >> 1) * CHUNK + (rows & 1) * 4 + rows // half_tokens)
    before = one_hot((rows + ROWS - jnp.where((rows & 3) == 0, 5, 1)) % ROWS)
    after = one_hot((rows + jnp.where((rows & 3) == 3, 5, 1)) % ROWS)

    def pack(src, dst, h):
        flat = src[:, pl.ds(h * half_tokens, half_tokens), :].reshape(ROWS, channels)
        dst[h] = dot(to_chunks, flat).astype(BF16).reshape(GROUP, CHUNK, channels)

    def exchange_copy(a, src, dst, h, k):
        to = partner_of(me, k)
        return pltpu.make_async_remote_copy(
            src_ref=src.at[h, to],
            dst_ref=dst.at[h, me],
            send_sem=send_sem.at[a, k],
            recv_sem=recv_sem.at[a, k],
            device_id=(to, tile),
            device_id_type=MESH,
        )

    def arrival(a, src, dst, h, k):
        origin = source_of(me, k)
        return pltpu.make_async_remote_copy(
            src_ref=src.at[h, origin],
            dst_ref=dst.at[h, origin],
            send_sem=send_sem.at[a, k],
            recv_sem=recv_sem.at[a, k],
            device_id=(origin, tile),
            device_id_type=MESH,
        )

    def send(a, src, dst, h):
        if comm:
            for k in range(GROUP - 1, 0, -1):
                exchange_copy(a, src, dst, h, k).start()
        dst[h, me] = src[h, me]

    def receive(a, src, dst, h):
        if comm:
            for k in range(GROUP - 1, 0, -1):
                arrival(a, src, dst, h, k).wait_recv()

    def small_copy(a, src, dst, slot, k, to):
        return pltpu.make_async_remote_copy(
            src_ref=src,
            dst_ref=dst.at[slot],
            send_sem=send_sem.at[a, k],
            recv_sem=recv_sem.at[a, k],
            device_id=to,
            device_id_type=MESH,
        )

    loads[0].wait()
    pack(tok_in, tsend, 0)
    loads[1].wait()
    parts = []
    for f in range(cot_in.shape[0]):
        frame = cot_in[f].astype(F32)
        parts.append(jnp.sum(frame * frame, axis=0, keepdims=True))
    squares = jnp.concatenate(parts + parts, axis=0)
    lanes_sum = squares[:, :128]
    for c in range(128, channels, 128):
        lanes_sum = lanes_sum + squares[:, c : c + 128]
    esend[...] = lanes_sum
    if comm:
        pl.semaphore_wait(barrier, 2 * (GROUP - 1))
        for k in range(1, GROUP):
            small_copy(6, esend, erecv, tile, k, (me, (tile + k) % GROUP)).start()
    erecv[tile] = esend[...]
    send(0, tsend, trecv, 0)
    pack(tok_in, tsend, 1)
    send(1, tsend, trecv, 1)
    pack(cot_in, csend, 0)
    if comm:
        for k in range(1, GROUP):
            small_copy(6, esend, erecv, (tile + GROUP - k) % GROUP, k, (me, (tile + k) % GROUP)).wait_recv()
    energy = erecv[0]
    for t in range(1, GROUP):
        energy = energy + erecv[t]
    energy = jnp.sum(energy, axis=1, keepdims=True)
    count = tok_in.shape[1] * GROUP * channels
    fsend[...] = jnp.broadcast_to(lax.rsqrt(energy / count + 1e-06), fsend.shape)
    if comm:
        for k in range(1, GROUP):
            small_copy(7, fsend, frecv, me, k, (partner_of(me, k), tile)).start()
    frecv[me] = fsend[...]
    send(2, csend, crecv, 0)
    pack(cot_in, csend, 1)
    send(3, csend, crecv, 1)

    same_token = ((row_index() >> 2) & 1) == ((lax.broadcasted_iota(jnp.int32, (ROWS, ROWS), 1) >> 2) & 1)
    closed = jnp.where(same_token, 0.0, -1e30).astype(F32)
    closed = jnp.concatenate([closed, closed], axis=1)
    step = 256

    for h in range(HALVES):
        receive(h, tsend, trecv, h)
        for c in range(0, channels, step):
            cols = slice(c, c + step)
            x = trecv[h, :, :, cols].reshape(ROWS, step)
            prev, succ, here = dot(before, x), dot(after, x), x.astype(F32)
            mixed = taps_ref[0:1, cols] * prev + taps_ref[1:2, cols] * here + taps_ref[2:3, cols] * succ
            hid[h, :, cols] = (here + mixed + bias_ref[:, cols]).astype(BF16)
        if h == 0:
            for load in loads[2:]:
                load.wait()
        for i in range(3):
            for c in range(0, channels, step):
                cols = slice(c, c + step)
                block = dot(hid[h], w[i, :, cols])
                if i == 0:
                    block = block * SCALE
                qkv[i, h, :, cols] = block.astype(BF16)
        for m in range(channels // PAIR):
            cols = slice(m * PAIR, (m + 1) * PAIR)
            qs = stacked(qkv[0, h, :, cols])
            qs_all[h, m] = qs
            scores = dot(qkv[1, h, :, cols], qs, ((1,), (1,))) + closed
            expo = jnp.exp(scores - jnp.max(scores, axis=0, keepdims=True))
            probs[h, m] = expo / jnp.sum(expo, axis=0, keepdims=True)

    for h in range(HALVES):
        if comm and h == 0:
            for k in range(1, GROUP):
                small_copy(7, fsend, frecv, source_of(me, k), k, (source_of(me, k), tile)).wait_recv()
        receive(2 + h, csend, crecv, h)
        factor = frecv[...].reshape(ROWS, 128)
        for m in range(channels // PAIR):
            cols = slice(m * PAIR, (m + 1) * PAIR)
            grad_out = (crecv[h, :, :, cols].reshape(ROWS, PAIR).astype(F32) * factor).astype(BF16)
            gs = stacked(grad_out)
            grad_prob = dot(qkv[2, h, :, cols], gs, ((1,), (1,)))
            prob = probs[h, m]
            low = prob.astype(BF16)
            delta = jnp.sum(low.astype(F32) * grad_prob, axis=0, keepdims=True)
            grad_scores = (prob * (grad_prob - delta)).astype(BF16)
            grads[2, h, :, cols] = dot(low, gs).astype(BF16)
            grads[1, h, :, cols] = dot(grad_scores, qs_all[h, m]).astype(BF16)
            both = dot(grad_scores, qkv[1, h, :, cols], ((0,), (0,)))
            lanes = lax.broadcasted_iota(jnp.int32, (ROWS, PAIR), 1)
            grads[0, h, :, cols] = (jnp.where(lanes < HEAD_DIM, both[:ROWS], both[ROWS:]) * SCALE).astype(BF16)
        for c in range(0, channels, step):
            cols = slice(c, c + step)
            total = dot(grads[0, h], w[0, cols, :], ((1,), (1,)))
            total = total + dot(grads[1, h], w[1, cols, :], ((1,), (1,)))
            total = total + dot(grads[2, h], w[2, cols, :], ((1,), (1,)))
            x = total.astype(BF16)
            prev, succ, here = dot(before, x), dot(after, x), x.astype(F32)
            back = here + taps_ref[0:1, cols] * succ + taps_ref[1:2, cols] * here + taps_ref[2:3, cols] * prev
            gsend[h, :, :, cols] = back.astype(BF16).reshape(GROUP, CHUNK, step)
        send(4 + h, gsend, grecv, h)

    for h in range(HALVES):
        receive(4 + h, gsend, grecv, h)
        flat = dot(from_chunks, grecv[h].reshape(ROWS, channels)).astype(BF16)
        out_ref[:, pl.ds(h * half_tokens, half_tokens), :] = flat.reshape(out_ref.shape[0], half_tokens, channels)

    if comm:
        for h in range(HALVES):
            for a, src, dst in ((0, tsend, trecv), (2, csend, crecv), (4, gsend, grecv)):
                for k in range(GROUP - 1, 0, -1):
                    exchange_copy(a + h, src, dst, h, k).wait_send()
        for k in range(1, GROUP):
            small_copy(6, esend, erecv, tile, k, (me, (tile + k) % GROUP)).wait_send()
            small_copy(7, fsend, frecv, me, k, (partner_of(me, k), tile)).wait_send()


def shards(comm, tokens, cotangent, w_query, w_key, w_value, conv_taps, conv_bias):
    frames, toks, channels = tokens.shape
    pairs = channels // PAIR
    exchange = pltpu.VMEM((HALVES, GROUP, CHUNK, channels), BF16)
    hbm, vmem = pl.BlockSpec(memory_space=pl.ANY), pl.BlockSpec(memory_space=pltpu.VMEM)
    return pl.pallas_call(
        functools.partial(kernel, comm),
        out_shape=jax.ShapeDtypeStruct((frames, toks, channels), BF16),
        in_specs=[hbm, hbm, hbm, hbm, hbm, vmem, vmem],
        out_specs=vmem,
        scratch_shapes=[
            pltpu.VMEM((frames, toks, channels), BF16),
            pltpu.VMEM((frames, toks, channels), BF16),
            pltpu.VMEM((3, channels, channels), BF16),
            exchange,
            exchange,
            exchange,
            exchange,
            exchange,
            exchange,
            pltpu.VMEM((8, 128), F32),
            pltpu.VMEM((GROUP, 8, 128), F32),
            pltpu.VMEM((8, 128), F32),
            pltpu.VMEM((GROUP, 8, 128), F32),
            pltpu.VMEM((HALVES, ROWS, channels), BF16),
            pltpu.VMEM((3, HALVES, ROWS, channels), BF16),
            pltpu.VMEM((HALVES, pairs, 2 * ROWS, PAIR), BF16),
            pltpu.VMEM((HALVES, pairs, ROWS, 2 * ROWS), F32),
            pltpu.VMEM((3, HALVES, ROWS, channels), BF16),
            pltpu.VMEM((8, 128), BF16),
            pltpu.SemaphoreType.DMA((5,)),
            pltpu.SemaphoreType.DMA((8, GROUP)),
            pltpu.SemaphoreType.DMA((8, GROUP)),
        ],
        compiler_params=pltpu.CompilerParams(
            collective_id=0, has_side_effects=True, vmem_limit_bytes=56 << 20
        ),
    )(tokens, cotangent, w_query, w_key, w_value, conv_taps, conv_bias.reshape(1, channels))


def solution(mesh, comm=True):
    in_specs = (P("orbit", "tile", None), P("orbit", "tile", None), P(), P(), P(), P(), P())
    out_specs = P("orbit", "tile", None)
    return jax.shard_map(
        functools.partial(shards, comm), mesh=mesh, in_specs=in_specs, out_specs=out_specs, check_vma=False
    )
```

```python
import functools

import jax
import jax.numpy as jnp
from jax import lax
from jax.experimental import pallas as pl
from jax.experimental.pallas import tpu as pltpu
from jax.sharding import PartitionSpec as P

MESH = pl.DeviceIdType.MESH
HEAD_DIM = 64
PAIR = 2 * HEAD_DIM
SCALE = HEAD_DIM**-0.5
GROUP = 16
HALVES = 2
CHUNK = 8
HUB = 1
SPLITS = ((0, 768), (768, 1280))
ROWS = GROUP * CHUNK
BF16 = jnp.bfloat16
F32 = jnp.float32


def partner_of(me, k):
    core, x, y = me % 2, (me // 2) % 4, me // 8
    return ((y + k // 8) % 2) * 8 + ((x + (k // 2) % 4) % 4) * 2 + (core + k % 2) % 2


def source_of(me, k):
    core, x, y = me % 2, (me // 2) % 4, me // 8
    return ((y + k // 8) % 2) * 8 + ((x + 4 - (k // 2) % 4) % 4) * 2 + (core + k % 2) % 2


def one_hot(source):
    columns = lax.broadcasted_iota(jnp.int32, (ROWS, ROWS), 1)
    return jnp.where(columns == source, 1.0, 0.0).astype(BF16)


def row_index():
    return lax.broadcasted_iota(jnp.int32, (ROWS, ROWS), 0)


def dot(a, b, dims=((1,), (0,))):
    return lax.dot_general(a, b, (dims, ((), ())), preferred_element_type=F32)


def stacked(block):
    lanes = lax.broadcasted_iota(jnp.int32, block.shape, 1)
    zero = jnp.zeros_like(block)
    return jnp.concatenate(
        [jnp.where(lanes < HEAD_DIM, block, zero), jnp.where(lanes < HEAD_DIM, zero, block)], axis=0
    )


def kernel(
    comm,
    tokens_hbm,
    cot_hbm,
    wq_hbm,
    wk_hbm,
    wv_hbm,
    taps_ref,
    bias_ref,
    out_ref,
    tok_in,
    cot_in,
    w,
    wt,
    tsend,
    trecv,
    csend,
    crecv,
    gsend,
    grecv,
    esend,
    erecv,
    hsend,
    hrecv,
    fsend,
    frecv,
    hid,
    qkv,
    qs_all,
    probs,
    grads,
    load_sem,
    send_sem,
    recv_sem,
    small_send,
    small_recv,
    go_sem,
):
    me = lax.axis_index("orbit")
    tile = lax.axis_index("tile")
    channels = tok_in.shape[-1]
    barrier = pltpu.get_barrier_semaphore()

    pending = []

    def launch(copy):
        copy.start()
        pending.append(copy)

    def drain():
        for copy in pending:
            copy.wait_send()

    loads = [
        pltpu.make_async_copy(tokens_hbm, tok_in, load_sem.at[0]),
        pltpu.make_async_copy(cot_hbm, cot_in, load_sem.at[1]),
        pltpu.make_async_copy(wq_hbm, w.at[0], load_sem.at[2]),
        pltpu.make_async_copy(wk_hbm, w.at[1], load_sem.at[3]),
        pltpu.make_async_copy(wv_hbm, w.at[2], load_sem.at[4]),
    ]
    for load in loads[:2]:
        load.start()
    if comm:
        for k in range(1, GROUP):
            peer = (me + k) % GROUP

            @pl.when(peer != HUB)
            def _():
                pl.semaphore_signal(barrier, inc=1, device_id=(peer, tile), device_id_type=MESH)

        @pl.when(me == HUB)
        def _():
            for k in range(1, GROUP):
                pl.semaphore_signal(barrier, inc=1, device_id=(me, (tile + k) % GROUP), device_id_type=MESH)

    rows = row_index()
    half_tokens = tok_in.shape[1] // HALVES
    to_chunks = one_hot((rows & 3) * half_tokens + (rows >> 3) * 2 + ((rows >> 2) & 1))
    from_chunks = one_hot(((rows % half_tokens) >> 1) * CHUNK + (rows & 1) * 4 + rows // half_tokens)
    before = one_hot((rows + ROWS - jnp.where((rows & 3) == 0, 5, 1)) % ROWS)
    after = one_hot((rows + jnp.where((rows & 3) == 3, 5, 1)) % ROWS)

    def pack(src, dst, h):
        flat = src[:, pl.ds(h * half_tokens, half_tokens), :].reshape(ROWS, channels)
        dst[h] = dot(to_chunks, flat).astype(BF16).reshape(GROUP, CHUNK, channels)

    def exchange_copy(a, src, dst, h, k, cols=slice(None)):
        to = partner_of(me, k)
        return pltpu.make_async_remote_copy(
            src_ref=src.at[h, to, :, cols],
            dst_ref=dst.at[h, me, :, cols],
            send_sem=send_sem.at[a, k],
            recv_sem=recv_sem.at[a, k],
            device_id=(to, tile),
            device_id_type=MESH,
        )

    def arrival(a, src, dst, h, k, cols=slice(None)):
        origin = source_of(me, k)
        return pltpu.make_async_remote_copy(
            src_ref=src.at[h, origin, :, cols],
            dst_ref=dst.at[h, origin, :, cols],
            send_sem=send_sem.at[a, k],
            recv_sem=recv_sem.at[a, k],
            device_id=(origin, tile),
            device_id_type=MESH,
        )

    def send(a, src, dst, h, cols=slice(None)):
        if comm:
            for k in range(GROUP - 1, 0, -1):
                launch(exchange_copy(a, src, dst, h, k, cols))
        dst[h, me, :, cols] = src[h, me, :, cols]

    def receive(a, src, dst, h, cols=slice(None)):
        if comm:
            for k in range(GROUP - 1, 0, -1):
                arrival(a, src, dst, h, k, cols).wait_recv()

    def small_copy(a, src, dst, k, to):
        return pltpu.make_async_remote_copy(
            src_ref=src,
            dst_ref=dst,
            send_sem=small_send.at[a, k],
            recv_sem=small_recv.at[a, k],
            device_id=to,
            device_id_type=MESH,
        )

    step = 256

    def transpose_weight(i):
        loads[2 + i].wait()
        for c in range(0, channels, step):
            wt[i, :, c : c + step] = w[i, c : c + step, :].T

    def local_energy():
        return small_copy(0, esend, erecv.at[me], me, (HUB, tile))

    def hub_energy(k):
        return small_copy(1, hsend, hrecv.at[tile], k, (me, (tile + k) % GROUP))

    def hub_factor(k):
        return small_copy(2, fsend, frecv, k, ((me + k) % GROUP, tile))

    def send_local_energy():
        if comm:

            @pl.when(me != HUB)
            def _():
                local_energy().start()

        @pl.when(me == HUB)
        def _():
            erecv[me] = esend[...]

    def send_hub_energy():
        @pl.when(me == HUB)
        def _():
            if comm:
                for k in range(1, GROUP):
                    peer = (me + k) % GROUP
                    small_copy(0, esend, erecv.at[peer], peer, (peer, tile)).wait_recv()
                pl.semaphore_wait(barrier, GROUP - 1)
            sums = jnp.sum(erecv[...].reshape(ROWS, 128), axis=1, keepdims=True)
            hsend[...] = jnp.broadcast_to(sums, (ROWS, 128)).T[:8]
            hrecv[tile] = hsend[...]
            if comm:
                for k in range(1, GROUP):
                    hub_energy(k).start()

    def send_factor():
        @pl.when(me == HUB)
        def _():
            if comm:
                for k in range(1, GROUP):
                    peer = (tile + GROUP - k) % GROUP
                    small_copy(1, hsend, hrecv.at[peer], k, (me, peer)).wait_recv()
            energy = hrecv[0]
            for t in range(1, GROUP):
                energy = energy + hrecv[t]
            count = tok_in.shape[1] * GROUP * channels
            fsend[...] = lax.rsqrt(energy / count + 1e-06)
            frecv[...] = fsend[...]
            if comm:
                for k in range(1, GROUP):
                    hub_factor(k).start()

    def receive_factor():
        if comm:

            @pl.when(me != HUB)
            def _():
                small_copy(2, fsend, frecv, (me + GROUP - HUB) % GROUP, (HUB, tile)).wait_recv()
                local_energy().wait_send()

            @pl.when(me == HUB)
            def _():
                for k in range(1, GROUP):
                    hub_energy(k).wait_send()
                    hub_factor(k).wait_send()

    loads[0].wait()
    pack(tok_in, tsend, 0)
    loads[1].wait()
    parts = []
    for f in range(cot_in.shape[0]):
        frame = cot_in[f].astype(F32)
        parts.append(jnp.sum(frame * frame, axis=0, keepdims=True))
    squares = jnp.concatenate(parts + parts, axis=0)
    lanes_sum = squares[:, :128]
    for c in range(128, channels, 128):
        lanes_sum = lanes_sum + squares[:, c : c + 128]
    esend[...] = lanes_sum
    for load in loads[2:]:
        load.start()
    if comm:

        @pl.when(me != HUB)
        def _():
            pl.semaphore_wait(barrier, GROUP - 1)

        @pl.when(me == HUB - 1)
        def _():
            pl.semaphore_signal(go_sem, inc=1, device_id=(HUB, tile), device_id_type=MESH)

        @pl.when(me == HUB)
        def _():
            pl.semaphore_wait(go_sem, 1)

    send_local_energy()
    send_hub_energy()
    send(0, tsend, trecv, 0)
    pack(tok_in, tsend, 1)
    send(1, tsend, trecv, 1)
    pack(cot_in, csend, 0)
    pack(cot_in, csend, 1)
    transpose_weight(0)
    transpose_weight(1)
    transpose_weight(2)
    send(2, csend, crecv, 0)

    same_token = ((row_index() >> 2) & 1) == ((lax.broadcasted_iota(jnp.int32, (ROWS, ROWS), 1) >> 2) & 1)
    closed = jnp.where(same_token, 0.0, -1e30).astype(F32)
    closed = jnp.concatenate([closed, closed], axis=1)
    for h in range(HALVES):
        receive(h, tsend, trecv, h)
        for c in range(0, channels, step):
            cols = slice(c, c + step)
            x = trecv[h, :, :, cols].reshape(ROWS, step)
            prev, succ, here = dot(before, x), dot(after, x), x.astype(F32)
            mixed = taps_ref[0:1, cols] * prev + taps_ref[1:2, cols] * here + taps_ref[2:3, cols] * succ
            hid[h, :, cols] = (here + mixed + bias_ref[cols].reshape(1, step)).astype(BF16)
        for i in range(3):
            for c in range(0, channels, step):
                cols = slice(c, c + step)
                block = dot(hid[h], w[i, :, cols])
                if i == 0:
                    block = block * SCALE
                qkv[i, h, :, cols] = block.astype(BF16)
        for m in range(channels // PAIR):
            cols = slice(m * PAIR, (m + 1) * PAIR)
            qs = stacked(qkv[0, h, :, cols])
            qs_all[h, m] = qs
            scores = dot(qkv[1, h, :, cols], qs, ((1,), (1,))) + closed
            expo = jnp.exp(scores - jnp.max(scores, axis=0, keepdims=True))
            probs[h, m] = expo / jnp.sum(expo, axis=0, keepdims=True)
        if h == 0:
            send_factor()
            send(3, csend, crecv, 1)

    for h in range(HALVES):
        if h == 0:
            receive_factor()
            factor = jnp.broadcast_to(frecv[0:1], (ROWS, 128)).T
        receive(2 + h, csend, crecv, h)
        for m in range(channels // PAIR):
            cols = slice(m * PAIR, (m + 1) * PAIR)
            grad_out = (crecv[h, :, :, cols].reshape(ROWS, PAIR).astype(F32) * factor).astype(BF16)
            gs = stacked(grad_out)
            grad_prob = dot(qkv[2, h, :, cols], gs, ((1,), (1,)))
            prob = probs[h, m]
            low = prob.astype(BF16)
            delta = jnp.sum(low.astype(F32) * grad_prob, axis=0, keepdims=True)
            grad_scores = (prob * (grad_prob - delta)).astype(BF16)
            grads[2, h, :, cols] = dot(low, gs).astype(BF16)
            grads[1, h, :, cols] = dot(grad_scores, qs_all[h, m]).astype(BF16)
            both = dot(grad_scores, qkv[1, h, :, cols], ((0,), (0,)))
            lanes = lax.broadcasted_iota(jnp.int32, (ROWS, PAIR), 1)
            grads[0, h, :, cols] = (jnp.where(lanes < HEAD_DIM, both[:ROWS], both[ROWS:]) * SCALE).astype(BF16)
        for c in range(0, channels, step):
            cols = slice(c, c + step)
            total = dot(grads[0, h], wt[0, :, cols])
            total = total + dot(grads[1, h], wt[1, :, cols])
            total = total + dot(grads[2, h], wt[2, :, cols])
            x = total.astype(BF16)
            prev, succ, here = dot(before, x), dot(after, x), x.astype(F32)
            back = here + taps_ref[0:1, cols] * succ + taps_ref[1:2, cols] * here + taps_ref[2:3, cols] * prev
            gsend[h, :, :, cols] = back.astype(BF16).reshape(GROUP, CHUNK, step)
            for part, (first, last) in enumerate(SPLITS):
                if c + step == last:
                    send(4 + 2 * h + part, gsend, grecv, h, slice(first, last))

    for h in range(HALVES):
        for part, (first, last) in enumerate(SPLITS):
            cols = slice(first, last)
            receive(4 + 2 * h + part, gsend, grecv, h, cols)
            flat = dot(from_chunks, grecv[h, :, :, cols].reshape(ROWS, last - first)).astype(BF16)
            toks = pl.ds(h * half_tokens, half_tokens)
            out_ref[:, toks, cols] = flat.reshape(out_ref.shape[0], half_tokens, last - first)

    drain()


def shards(comm, tokens, cotangent, w_query, w_key, w_value, conv_taps, conv_bias):
    frames, toks, channels = tokens.shape
    pairs = channels // PAIR
    exchange = pltpu.VMEM((HALVES, GROUP, CHUNK, channels), BF16)
    hbm, vmem = pl.BlockSpec(memory_space=pl.ANY), pl.BlockSpec(memory_space=pltpu.VMEM)
    return pl.pallas_call(
        functools.partial(kernel, comm),
        out_shape=pltpu.VMEM((frames, toks, channels), BF16),
        in_specs=[hbm, hbm, hbm, hbm, hbm, vmem, vmem],
        out_specs=vmem,
        scratch_shapes=[
            pltpu.VMEM((frames, toks, channels), BF16),
            pltpu.VMEM((frames, toks, channels), BF16),
            pltpu.VMEM((3, channels, channels), BF16),
            pltpu.VMEM((3, channels, channels), BF16),
            exchange,
            exchange,
            exchange,
            exchange,
            exchange,
            exchange,
            pltpu.VMEM((8, 128), F32),
            pltpu.VMEM((GROUP, 8, 128), F32),
            pltpu.VMEM((8, 128), F32),
            pltpu.VMEM((GROUP, 8, 128), F32),
            pltpu.VMEM((8, 128), F32),
            pltpu.VMEM((8, 128), F32),
            pltpu.VMEM((HALVES, ROWS, channels), BF16),
            pltpu.VMEM((3, HALVES, ROWS, channels), BF16),
            pltpu.VMEM((HALVES, pairs, 2 * ROWS, PAIR), BF16),
            pltpu.VMEM((HALVES, pairs, ROWS, 2 * ROWS), F32),
            pltpu.VMEM((3, HALVES, ROWS, channels), BF16),
            pltpu.SemaphoreType.DMA((5,)),
            pltpu.SemaphoreType.DMA((8, GROUP)),
            pltpu.SemaphoreType.DMA((8, GROUP)),
            pltpu.SemaphoreType.DMA((3, GROUP)),
            pltpu.SemaphoreType.DMA((3, GROUP)),
            pltpu.SemaphoreType.REGULAR,
        ],
        compiler_params=pltpu.CompilerParams(
            collective_id=0, has_side_effects=True, vmem_limit_bytes=58 << 20
        ),
    )(tokens, cotangent, w_query, w_key, w_value, conv_taps, conv_bias)


def solution(mesh, comm=True):
    in_specs = (P("orbit", "tile", None), P("orbit", "tile", None), P(), P(), P(), P(), P())
    out_specs = P("orbit", "tile", None)
    return jax.shard_map(
        functools.partial(shards, comm), mesh=mesh, in_specs=in_specs, out_specs=out_specs, check_vma=False
    )
```
